512 devices in a mesh: dp: 64 (over x, z, core), tensor: 8 (over y).
Axes of the slice: x: 4, y: 8, z: 8, core: 2. Of those that a mesh axis runs over, the one named last changes fastest.
Arguments:
- activations: bfloat16 [49152, 4096], P('dp'), may hold values from -16 to 16
- grad_out: bfloat16 [49152, 2, 1024], P('dp', None, 'tensor'), may hold values from -0.059814453 to 0.059814453
- weights: float32 [4096, 2, 1024], P('dp', None, 'tensor')
- first_moment: float32 [4096, 2, 1024], P('dp', None, 'tensor'), may hold values from -6 to 6
- second_moment: float32 [4096, 2, 1024], P('dp', None, 'tensor')
- step: int32 [1], replicated, may hold values from 1 to 40
Outputs:
- new_weights: float32 [4096, 2, 1024], P('dp', None, 'tensor')
- new_first: float32 [4096, 2, 1024], P('dp', None, 'tensor')
- new_second: float32 [4096, 2, 1024], P('dp', None, 'tensor')
- ratios: float32 [2], replicated
- new_kv: bfloat16 [49152, 2, 1024], P('dp', None, 'tensor')
The draws below stay inside these ranges and needn't reach their ends.
All inputs are finite; a program needn't handle non-finite values.
Results may differ from the reference program's by a relative error of at most 0.001.
The reference program's roundings to bfloat16 on the way (of `half_weights`) count: a program that leaves them out, or rounds other values in their place, can miss the bound.
Values may be sent and summed in bfloat16 or wider, within the bound.
A program may use at most 64 MiB of HBM per device.

```python
import math
import jax
import jax.numpy as jnp
from jax import lax

D = 4096
KVW = 1024
TOKENS = 49152


def factor_line(key, count, rise):
    spread = jax.random.uniform(key, (count,), jnp.float32)
    place = jnp.arange(count, dtype=jnp.float32) / (count - 1)
    return jnp.power(10.0, spread - 0.5) * jnp.power(rise, place - 0.5)


def draw_weights(key, part):
    rise = 1.7320508
    base = jax.random.normal(jax.random.fold_in(key, 11), (D, 2, KVW), jnp.float32)
    row_scale = factor_line(jax.random.fold_in(key, 12), D, rise)
    col_scale = factor_line(jax.random.fold_in(key, 13), KVW, rise)
    return base * row_scale[:, None, None] * col_scale[None, None, :]


def draw_second_moment(key, part):
    rise = 3.0
    base = jax.random.uniform(jax.random.fold_in(key, 21), (D, 2, KVW), jnp.float32, 0.5, 2.0)
    row_scale = factor_line(jax.random.fold_in(key, 22), D, rise)
    col_scale = factor_line(jax.random.fold_in(key, 23), KVW, rise)
    return 0.5 * base / (row_scale[:, None, None] * col_scale[None, None, :])


def with_spikes(drawn, own_key, source, target, parts, factor):
    owner, partner = [(jnp.arange(drawn.shape[dim]) // (drawn.shape[dim] // parts)).reshape([-1 if axis == dim else 1 for axis in range(drawn.ndim)]) for dim in (source, target)]
    chosen = jax.random.permutation(own_key, parts)[partner]
    strong = (owner == chosen) | (owner == (partner + parts // 2) % parts)
    return jnp.where(strong, factor * drawn, drawn)


def steps_of(stream_key, shape, pieces, low, largest):
    def one(axis_at, parts):
        heights = jax.random.uniform(jax.random.fold_in(jax.random.fold_in(stream_key, 6), axis_at), (parts,), jnp.float32, low / len(pieces), largest / len(pieces))
        return jnp.repeat(jnp.exp(heights), shape[axis_at] // parts).reshape((-1,) + (1,) * (len(shape) - axis_at - 1))

    loudness = one(*pieces[0])
    for cut in pieces[1:]:
        loudness = loudness * one(*cut)
    return loudness


def noise(own_key, dims, scale, most, split=(), kind=jnp.bfloat16):
    factor_of = steps_of(own_key, dims, split, -0.22, 0.18) if split else 1.0
    array = jax.random.normal(own_key, dims, jnp.float32) * scale * factor_of
    return jnp.minimum(jnp.maximum(array, -most), most).astype(kind)


def noise_with(rng, shape, width, reach, split, heavy, kind=jnp.bfloat16):
    entries = width * jax.random.normal(rng, shape, jnp.float32)
    if split:
        entries = entries * steps_of(rng, shape, split, -0.22, 0.18)
    return jnp.clip(with_spikes(entries, jax.random.fold_in(rng, 3), *heavy), -reach, reach).astype(kind)


def setup_inputs(seed: int = 0) -> dict:
    splits = jax.random.split(jax.random.key(seed), 7)
    return {
        "activations": noise_with(splits[0], (TOKENS, D), 1.0, 16.0, ((0, 64),), (0, 1, 64, 4.0)),
        "grad_out": noise(splits[1], (TOKENS, 2, KVW), 0.01, 0.059814453, ((0, 64), (2, 8))),
        "weights": draw_weights(jax.random.fold_in(splits[6], 71), 0),
        "first_moment": noise(splits[3], (D, 2, KVW), 1.0, 6.0, ((0, 64), (2, 8)), jnp.float32),
        "second_moment": draw_second_moment(jax.random.fold_in(splits[6], 71), 0),
        "step": jax.random.randint(splits[5], (1,), 1, 41).astype(jnp.int32),
    }


def reference(activations, grad_out, weights, first_moment, second_moment, step):
    inputs = activations.astype(jnp.float32)
    grad = jnp.einsum('td,tsc->dsc', inputs, grad_out.astype(jnp.float32))
    new_first = 0.9 * first_moment + 0.1 * grad
    new_second = 0.95 * second_moment + 0.05 * grad * grad
    count = step[0].astype(jnp.float32)
    bias_one = 1.0 - jnp.exp(count * math.log(0.9))
    bias_two = 1.0 - jnp.exp(count * math.log(0.95))
    update = new_first / bias_one / (jnp.sqrt(new_second / bias_two) + 1e-06) + 0.1 * weights
    weight_sq = lax.optimization_barrier(jnp.sum(weights * weights, axis=(0, 2)))
    update_sq = lax.optimization_barrier(jnp.sum(update * update, axis=(0, 2)))
    ratios = jnp.sqrt(weight_sq) / (jnp.sqrt(update_sq) + 1e-06)
    new_weights = weights - 0.05 * ratios[None, :, None] * update
    half_weights = new_weights.astype(jnp.bfloat16)
    new_kv = jnp.einsum('td,dsc->tsc', inputs, half_weights.astype(jnp.float32)).astype(jnp.bfloat16)
    return (new_weights, new_first, new_second, ratios, new_kv)
```

```python
import functools
import math

import jax
import jax.numpy as jnp
from jax import lax
from jax.experimental import pallas as pl
from jax.experimental.pallas import tpu as pltpu
from jax.sharding import PartitionSpec as P

NX, NZ, NC = 4, 8, 2
MESH = pl.DeviceIdType.MESH
TOP = 32767.0


def chunk_shift(k):
    half = NZ // 2
    return lax.select(lax.rem(k, 2) == 1, half - (k + 1) // 2, half + k // 2)


def near_shift(i):
    return lax.select(lax.rem(i, 2) == 1, (i + 1) // 2, lax.rem(NZ - i // 2, NZ))


def fresh(ny, rows, step_ref, act_hbm, gout_hbm, w_hbm, m_hbm, v_hbm,
          nw_ref, nm_ref, nv_ref, ratio_ref, kv_ref,
          act, gout, w_ref, m_ref, v_ref, g2, mm, crecv, xsend, xrecv, xssend, xsrecv, zsend, zrecv,
          upd, ar1, ar2, ar3, ag, acc,
          act_sem, in_sem, cs, cr, xs, xr, xss, xsr, zs, zr, a1s, a1r, a2s, a2r, a3s, a3r,
          gzs, gzr, gxs, gxr, gcs, gcr):
    dp, y = lax.axis_index("dp"), lax.axis_index("tensor")
    c = lax.rem(dp, NC)
    z = lax.rem(dp // NC, NZ)
    x = dp // (NC * NZ)
    wide = NC * rows
    f32 = jnp.float32

    def at(xx, zz, cc):
        return (xx * NZ + zz) * NC + cc

    def dev(index):
        return {"dp": index, "tensor": y}

    def remote(src, dst, send, recv, device):
        return pltpu.make_async_remote_copy(src_ref=src, dst_ref=dst, send_sem=send, recv_sem=recv,
                                            device_id=device, device_id_type=MESH)

    partner = dev(at(x, z, 1 - c))

    def xpeer(o):
        return dev(at(lax.rem(x + o, NX), z, c))

    def zpeer(o):
        return dev(at(x, lax.rem(z + o, NZ), c))

    barrier = pltpu.get_barrier_semaphore()

    def greet(device):
        pl.semaphore_signal(barrier, inc=1, device_id=device, device_id_type=MESH)

    mine1 = x * NC + c
    n1 = NX * NC

    def peer1(o):
        other = lax.rem(mine1 + o, n1)
        return dev(at(other // NC, z, lax.rem(other, NC)))

    for o in range(1, n1):
        greet(peer1(o))
    for o in range(1, NZ):
        greet(zpeer(o))
    for o in range(1, ny):
        greet({"dp": dp, "tensor": lax.rem(y + o, ny)})
    greeted = n1 - 1 + NZ - 1 + ny - 1

    load_g = pltpu.make_async_copy(gout_hbm, gout, in_sem.at[0])
    load_w = pltpu.make_async_copy(w_hbm, w_ref, in_sem.at[1])
    load_m = pltpu.make_async_copy(m_hbm, m_ref, in_sem.at[2])
    load_v = pltpu.make_async_copy(v_hbm, v_ref, in_sem.at[3])

    def strip(bx, k):
        zz = lax.rem(z + chunk_shift(k), NZ)
        return pl.ds(pl.multiple_of((bx * NZ + zz) * wide, wide), wide)

    def load_act(bx, k):
        return pltpu.make_async_copy(act_hbm.at[:, strip(bx, k)], act.at[:, strip(bx, k)], act_sem.at[k, bx])

    load_g.start()

    def start_loads(k, _):
        for bx in range(NX):
            load_act(bx, k).start()
        return 0

    lax.fori_loop(0, NZ, start_loads, 0)
    load_w.start()
    load_m.start()
    load_v.start()
    load_g.wait()
    half_c = g2.shape[1] // 2
    g2[:, :half_c] = gout[:, 0, :]
    g2[:, half_c:] = gout[:, 1, :]

    own_rows = pl.ds(pl.multiple_of(c * rows, rows), rows)
    other_rows = pl.ds(pl.multiple_of((1 - c) * rows, rows), rows)

    def core_copy(k):
        return remote(mm.at[k, :, other_rows, :], crecv.at[k], cs.at[k], cr.at[k], partner)

    def x_copy(k, o):
        return remote(xsend.at[k, o - 1], xrecv.at[k, o - 1], xs.at[k, o - 1], xr.at[k, o - 1], xpeer(o))

    def xscale_copy(k, o):
        return remote(xssend.at[k, o - 1], xsrecv.at[k, o - 1], xss.at[k, o - 1], xsr.at[k, o - 1], xpeer(o))

    def z_copy(k):
        return remote(zsend.at[k], zrecv.at[k], zs.at[k], zr.at[k], zpeer(chunk_shift(k)))

    def grads(k, _):
        @pl.when(k < NZ)
        def _():
            for bx in range(NX):
                load_act(bx, k).wait()
            left = jnp.concatenate([act[:, strip(bx, k)] for bx in range(NX)], axis=1)
            part = lax.dot_general(left, g2[...], (((0,), (0,)), ((), ())), preferred_element_type=f32)
            for bx in range(NX):
                mm[k, bx] = part[bx * wide:(bx + 1) * wide]

            @pl.when(k == 0)
            def _():
                pl.semaphore_wait(barrier, greeted)

            core_copy(k).start()

        @pl.when(k >= 1)
        def _():
            j = k - 1
            core_copy(j).wait_recv()
            for o in range(1, NX):
                bx = lax.rem(x + o, NX)
                value = mm[j, bx, own_rows, :] + crecv[j, bx]
                top = jnp.max(jnp.abs(value), axis=0, keepdims=True)
                xsend[j, o - 1] = jnp.round(value * (TOP / jnp.maximum(top, 1e-30))).astype(jnp.int32).astype(jnp.int16)
                xssend[j, o - 1] = top
                xscale_copy(j, o).start()
                x_copy(j, o).start()

        return 0

    lax.fori_loop(0, NZ + 1, grads, 0)

    def along_x(k, _):
        total = mm[k, x, own_rows, :] + crecv[k, x]
        for o in range(1, NX):
            xscale_copy(k, o).wait_recv()
            x_copy(k, o).wait_recv()
            total += xrecv[k, o - 1].astype(jnp.int32).astype(f32) * (xsrecv[k, o - 1] * (1.0 / TOP))
        zsend[k] = total

        @pl.when(k < NZ - 1)
        def _():
            z_copy(k).start()

        return 0

    lax.fori_loop(0, NZ, along_x, 0)

    load_w.wait()
    load_m.wait()
    load_v.wait()
    count = jnp.full((1, half_c), step_ref[0].astype(f32), f32)
    bias_one = 1.0 - jnp.exp(count * math.log(0.9))
    bias_two = 1.0 - jnp.exp(count * math.log(0.95))

    def along_z(k, total):
        z_copy(k).wait_recv()
        return total + zrecv[k]

    grad = lax.fori_loop(0, NZ - 1, along_z, zsend[NZ - 1])

    sums_u, sums_w = [], []
    for s in range(2):
        g = grad[:, s * half_c:(s + 1) * half_c]
        weight = w_ref[:, s, :]
        first = 0.9 * m_ref[:, s, :] + 0.1 * g
        second = 0.95 * v_ref[:, s, :] + 0.05 * g * g
        update = first / bias_one / (jnp.sqrt(second / bias_two) + 1e-06) + 0.1 * weight
        nm_ref[:, s, :] = first
        nv_ref[:, s, :] = second
        upd[s] = update
        sums_u.append(jnp.sum(update * update, axis=0, keepdims=True))
        sums_w.append(jnp.sum(weight * weight, axis=0, keepdims=True))
    tile = jnp.concatenate(sums_u + sums_w + [jnp.zeros((4, half_c), f32)], axis=0)

    def exchange(tile, ar, send, recv, n, me, device):
        ar[me] = tile
        copies = [remote(ar.at[me], ar.at[me], send.at[o], recv.at[o], device(o)) for o in range(1, n)]
        for copy in copies:
            copy.start()
        for copy in copies:
            copy.wait()
        total = ar[0]
        for i in range(1, n):
            total += ar[i]
        return total

    tile = exchange(tile, ar1, a1s, a1r, n1, mine1, peer1)
    tile = exchange(tile, ar2, a2s, a2r, NZ, z, zpeer)
    tile = exchange(tile, ar3, a3s, a3r, ny, y, lambda o: {"dp": dp, "tensor": lax.rem(y + o, ny)})
    norms = jnp.sqrt(jnp.sum(tile, axis=1, keepdims=True))
    ratio = norms[2:4] / (norms[0:2] + 1e-06)
    ratio_ref[...] = jnp.broadcast_to(ratio, ratio_ref.shape)
    for s in range(2):
        new = w_ref[:, s, :] - 0.05 * ratio[s:s + 1] * upd[s]
        nw_ref[:, s, :] = new
        ag[dp, :, s * half_c:(s + 1) * half_c] = new.astype(jnp.bfloat16)

    def gz_copy(i):
        return remote(ag.at[dp], ag.at[dp], gzs.at[i], gzr.at[i], zpeer(near_shift(i)))

    def held(i, p):
        return at(lax.rem(x - p + NX, NX), lax.rem(z - near_shift(i) + NZ, NZ), c)

    def gx_copy(i, p):
        block = held(i, 0)
        return remote(ag.at[block], ag.at[block], gxs.at[i, p], gxr.at[i, p], xpeer(p))

    def gc_copy(i, p):
        block = held(i, p)
        return remote(ag.at[block], ag.at[block], gcs.at[i, p], gcr.at[i, p], partner)

    def send_z(i, _):
        gz_copy(i).start()
        return 0

    lax.fori_loop(1, NZ, send_z, 0)

    def send_x(i, _):
        @pl.when(i > 0)
        def _():
            gz_copy(i).wait_recv()

        for p in (1, 3, 2)[:NX - 1] if NX == 4 else range(1, NX):
            gx_copy(i, p).start()
        gc_copy(i, 0).start()
        return 0

    lax.fori_loop(0, NZ, send_x, 0)
    acc[...] = jnp.zeros_like(acc)

    def product(i, _):
        @pl.when(i < NZ)
        def _():
            for p in range(1, NX):
                gx_copy(i, p).wait_recv()
                gc_copy(i, p).start()

        @pl.when(i >= 1)
        def _():
            j = i - 1
            for p in range(NX):
                gc_copy(j, p).wait_recv()
            zz = lax.rem(z - near_shift(j) + NZ, NZ)
            cols = [pl.ds(pl.multiple_of((bx * NZ + zz) * wide, wide), wide) for bx in range(NX)]
            left = jnp.concatenate([act[:, at_] for at_ in cols], axis=1)
            right = jnp.concatenate([ag[at(bx, zz, cc)] for bx in range(NX) for cc in range(NC)], axis=0)
            acc[...] += jnp.dot(left, right, preferred_element_type=f32)

        return 0

    lax.fori_loop(0, NZ + 1, product, 0)
    kv_ref[:, 0, :] = acc[:, :half_c].astype(jnp.bfloat16)
    kv_ref[:, 1, :] = acc[:, half_c:].astype(jnp.bfloat16)

    def drain(k, _):
        core_copy(k).wait_send()
        for o in range(1, NX):
            xscale_copy(k, o).wait_send()
            x_copy(k, o).wait_send()
            gx_copy(k, o).wait_send()
        for p in range(NX):
            gc_copy(k, p).wait_send()

        @pl.when(k < NZ - 1)
        def _():
            z_copy(k).wait_send()

        @pl.when(k > 0)
        def _():
            gz_copy(k).wait_send()

        return 0

    lax.fori_loop(0, NZ, drain, 0)


def local(ny, activations, grad_out, weights, first_moment, second_moment, step):
    tokens, d = activations.shape
    half_c = grad_out.shape[2]
    cols = 2 * half_c
    rows = d // (NX * NZ * NC)
    f32, bf16 = jnp.float32, jnp.bfloat16
    vmem, dma = pltpu.VMEM, pltpu.SemaphoreType.DMA
    any_, in_vmem = pl.BlockSpec(memory_space=pl.ANY), pl.BlockSpec(memory_space=pltpu.VMEM)
    state = jax.ShapeDtypeStruct((rows, 2, half_c), f32)
    nw, nm, nv, ratio, kv = pl.pallas_call(
        functools.partial(fresh, ny, rows),
        name="lamb_kv",
        out_shape=(state, state, state, jax.ShapeDtypeStruct((2, half_c), f32),
                   jax.ShapeDtypeStruct((tokens, 2, half_c), bf16)),
        in_specs=[pl.BlockSpec(memory_space=pltpu.SMEM)] + [any_] * 5,
        out_specs=(in_vmem,) * 5,
        scratch_shapes=[
            vmem((tokens, d), bf16),
            vmem((tokens, 2, half_c), bf16),
            vmem((rows, 2, half_c), f32),
            vmem((rows, 2, half_c), f32),
            vmem((rows, 2, half_c), f32),
            vmem((tokens, cols), bf16),
            vmem((NZ, NX, NC * rows, cols), f32),
            vmem((NZ, NX, rows, cols), f32),
            vmem((NZ, NX - 1, rows, cols), jnp.int16),
            vmem((NZ, NX - 1, rows, cols), jnp.int16),
            vmem((NZ, NX - 1, 1, cols), f32),
            vmem((NZ, NX - 1, 1, cols), f32),
            vmem((NZ, rows, cols), f32),
            vmem((NZ, rows, cols), f32),
            vmem((2, rows, half_c), f32),
            vmem((NX * NC, 8, half_c), f32),
            vmem((NZ, 8, half_c), f32),
            vmem((ny, 8, half_c), f32),
            vmem((NX * NZ * NC, rows, cols), bf16),
            vmem((tokens, cols), f32),
            dma((NZ, NX)), dma((4,)), dma((NZ,)), dma((NZ,)),
            dma((NZ, NX - 1)), dma((NZ, NX - 1)), dma((NZ, NX - 1)), dma((NZ, NX - 1)),
            dma((NZ,)), dma((NZ,)),
            dma((NX * NC,)), dma((NX * NC,)), dma((NZ,)), dma((NZ,)), dma((ny,)), dma((ny,)),
            dma((NZ,)), dma((NZ,)), dma((NZ, NX)), dma((NZ, NX)), dma((NZ, NX)), dma((NZ, NX)),
        ],
        compiler_params=pltpu.CompilerParams(collective_id=0, has_side_effects=True, vmem_limit_bytes=56 * 2**20),
    )(step, activations, grad_out, weights, first_moment, second_moment)
    return nw, nm, nv, ratio[:, 0], kv


def solution(mesh):
    in_specs = (
        P("dp", None),
        P("dp", None, "tensor"),
        P("dp", None, "tensor"),
        P("dp", None, "tensor"),
        P("dp", None, "tensor"),
        P(),
    )
    out_specs = (
        P("dp", None, "tensor"),
        P("dp", None, "tensor"),
        P("dp", None, "tensor"),
        P(),
        P("dp", None, "tensor"),
    )
    return jax.shard_map(functools.partial(local, mesh.shape["tensor"]), mesh=mesh, in_specs=in_specs,
                         out_specs=out_specs, check_vma=False)
```

```python
import functools
import math

import jax
import jax.numpy as jnp
from jax import lax
from jax.experimental import pallas as pl
from jax.experimental.pallas import tpu as pltpu
from jax.sharding import PartitionSpec as P

NX, NZ, NC = 4, 8, 2
MESH = pl.DeviceIdType.MESH
TOP = 32767.0
MEET, LAG = 0, 3
LAG_CORE = 2


def code(value):
    top = jnp.max(jnp.abs(value), axis=0, keepdims=True)
    return jnp.round(value * (TOP / jnp.maximum(top, 1e-30))).astype(jnp.int32).astype(jnp.int16), top


def decode(short, top):
    return short.astype(jnp.int32).astype(jnp.float32) * (top * (1.0 / TOP))


def chunk_shift(k):
    half = NZ // 2
    return lax.select(lax.rem(k, 2) == 1, half - (k + 1) // 2, half + k // 2)


def near_shift(i):
    return lax.select(lax.rem(i, 2) == 1, (i + 1) // 2, lax.rem(NZ - i // 2, NZ))


def fresh(ny, rows, step_ref, act_hbm, gout_hbm, w_hbm, m_hbm, v_hbm,
          nw_out, nm_out, nv_out, ratio_out, kv_out,
          nw_ref, nm_ref, nv_ref, ratio_ref, kv_ref,
          act, gout, w_ref, m_ref, v_ref, g2, mm, crecv, xsend, xrecv, xssend, xsrecv, zsend, zrecv, zssend, zsrecv, own,
          upd, wz, usend, ussend, uz, uzs, ar1, ar2, ar3, ag, acc,
          act_sem, in_sem, out_sem, cs, cr, xs, xr, xss, xsr, zs, zr, zss, zsr, a1s, a1r, a2s, a2r, a3s, a3r,
          ws, wr, us, ur, uss, usr, gxs, gxr, gcs, gcr):
    dp, y = lax.axis_index("dp"), lax.axis_index("tensor")
    c = lax.rem(dp, NC)
    z = lax.rem(dp // NC, NZ)
    x = dp // (NC * NZ)
    wide = NC * rows
    f32 = jnp.float32

    def at(xx, zz, cc):
        return (xx * NZ + zz) * NC + cc

    def dev(index):
        return {"dp": index, "tensor": y}

    def remote(src, dst, send, recv, device):
        return pltpu.make_async_remote_copy(src_ref=src, dst_ref=dst, send_sem=send, recv_sem=recv,
                                            device_id=device, device_id_type=MESH)

    partner = dev(at(x, z, 1 - c))

    def xpeer(o):
        return dev(at(lax.rem(x + o, NX), z, c))

    def zpeer(o):
        return dev(at(x, lax.rem(z + o, NZ), c))

    load_g = pltpu.make_async_copy(gout_hbm, gout, in_sem.at[0])
    load_w = pltpu.make_async_copy(w_hbm, w_ref, in_sem.at[1])
    load_m = pltpu.make_async_copy(m_hbm, m_ref, in_sem.at[2])
    load_v = pltpu.make_async_copy(v_hbm, v_ref, in_sem.at[3])

    def strip(bx, k):
        zz = lax.rem(z + chunk_shift(k), NZ)
        return pl.ds(pl.multiple_of((bx * NZ + zz) * wide, wide), wide)

    def load_act(bx, k):
        return pltpu.make_async_copy(act_hbm.at[:, strip(bx, k)], act.at[:, strip(bx, k)], act_sem.at[k, bx])

    load_g.start()

    def start_loads(k, _):
        for bx in range(NX):
            load_act(bx, k).start()
        return 0

    lax.fori_loop(0, NZ, start_loads, 0)
    load_w.start()
    load_m.start()
    load_v.start()
    barrier = pltpu.get_barrier_semaphore()

    def greet(device):
        pl.semaphore_signal(barrier, inc=1, device_id=device, device_id_type=MESH)

    mine1 = x * NC + c
    n1 = NX * NC

    def peer1(o):
        other = lax.rem(mine1 + o, n1)
        return dev(at(other // NC, z, lax.rem(other, NC)))

    for o in range(1, n1):
        greet(peer1(o))
    for o in range(1, NZ):
        greet(zpeer(o))
    for o in range(1, ny):
        greet({"dp": dp, "tensor": lax.rem(y + o, ny)})
    greeted = n1 - 1 + NZ - 1 + ny - 1

    load_g.wait()
    half_c = g2.shape[1] // 2
    g2[:, :half_c] = gout[:, 0, :]
    g2[:, half_c:] = gout[:, 1, :]

    own_rows = pl.ds(pl.multiple_of(c * rows, rows), rows)
    other_rows = pl.ds(pl.multiple_of((1 - c) * rows, rows), rows)

    def core_copy(k):
        return remote(mm.at[k, :, other_rows, :], crecv.at[k], cs.at[k], cr.at[k], partner)

    def x_copy(k, o):
        return remote(xsend.at[k, o - 1], xrecv.at[k, o - 1], xs.at[k, o - 1], xr.at[k, o - 1], xpeer(o))

    def xscale_copy(k, o):
        return remote(xssend.at[k, o - 1], xsrecv.at[k, o - 1], xss.at[k, o - 1], xsr.at[k, o - 1], xpeer(o))

    def z_copy(k):
        return remote(zsend.at[k], zrecv.at[k], zs.at[k], zr.at[k], zpeer(chunk_shift(k)))

    def zscale_copy(k):
        return remote(zssend.at[k], zsrecv.at[k], zss.at[k], zsr.at[k], zpeer(chunk_shift(k)))

    def w_copy(i):
        return remote(w_ref, wz.at[i], ws.at[i], wr.at[i], zpeer(near_shift(i)))

    def u_copy(i):
        return remote(usend, uz.at[i], us.at[i], ur.at[i], zpeer(near_shift(i)))

    def uscale_copy(i):
        return remote(ussend, uzs.at[i], uss.at[i], usr.at[i], zpeer(near_shift(i)))

    def grads(k, _):
        @pl.when(k < NZ)
        def _():
            for bx in range(NX):
                load_act(bx, k).wait()
            left = jnp.concatenate([act[:, strip(bx, k)] for bx in range(NX)], axis=1)
            part = lax.dot_general(left, g2[...], (((0,), (0,)), ((), ())), preferred_element_type=f32)
            for bx in range(NX):
                mm[k, bx] = part[bx * wide:(bx + 1) * wide]

            @pl.when(k == MEET)
            def _():
                pl.semaphore_wait(barrier, greeted)
                for j in range(MEET):
                    core_copy(j).start()

            @pl.when(k >= MEET)
            def _():
                core_copy(k).start()

            @pl.when(k == MEET)
            def _():
                load_w.wait()
                for i in range(1, NZ):
                    w_copy(i).start()

        @pl.when(k >= LAG)
        def _():
            j = k - LAG
            core_copy(j).wait_recv()
            for o in range(1, NX):
                bx = lax.rem(x + o, NX)
                xsend[j, o - 1], xssend[j, o - 1] = code(mm[j, bx, own_rows, :] + crecv[j, bx])
                xscale_copy(j, o).start()
                x_copy(j, o).start()

        return 0

    lax.fori_loop(0, NZ + LAG, grads, 0)

    def along_x(k, _):
        total = mm[k, x, own_rows, :] + crecv[k, x]
        for o in range(1, NX):
            xscale_copy(k, o).wait_recv()
            x_copy(k, o).wait_recv()
            total += decode(xrecv[k, o - 1], xsrecv[k, o - 1])

        @pl.when(k < NZ - 1)
        def _():
            zsend[k], zssend[k] = code(total)
            zscale_copy(k).start()
            z_copy(k).start()

        @pl.when(k == NZ - 1)
        def _():
            own[...] = total

        return 0

    lax.fori_loop(0, NZ, along_x, 0)

    load_m.wait()
    load_v.wait()
    count = jnp.full((1, half_c), step_ref[0].astype(f32), f32)
    bias_one = 1.0 - jnp.exp(count * math.log(0.9))
    bias_two = 1.0 - jnp.exp(count * math.log(0.95))

    def along_z(k, total):
        zscale_copy(k).wait_recv()
        z_copy(k).wait_recv()
        return total + decode(zrecv[k], zsrecv[k])

    grad = lax.fori_loop(0, NZ - 1, along_z, own[...])

    sums_u, sums_w = [], []
    for s in range(2):
        g = grad[:, s * half_c:(s + 1) * half_c]
        weight = w_ref[:, s, :]
        first = 0.9 * m_ref[:, s, :] + 0.1 * g
        second = 0.95 * v_ref[:, s, :] + 0.05 * g * g
        update = first / bias_one / (jnp.sqrt(second / bias_two) + 1e-06) + 0.1 * weight
        nm_ref[:, s, :] = first
        nv_ref[:, s, :] = second
        upd[s] = update
        sums_u.append(jnp.sum(update * update, axis=0, keepdims=True))
        sums_w.append(jnp.sum(weight * weight, axis=0, keepdims=True))
    puts = [pltpu.make_async_copy(a, b, out_sem.at[i]) for i, (a, b) in enumerate(
        ((nm_ref, nm_out), (nv_ref, nv_out), (nw_ref, nw_out), (ratio_ref, ratio_out), (kv_ref, kv_out)))]
    tile = jnp.concatenate(sums_u + sums_w + [jnp.zeros((4, half_c), f32)], axis=0)

    def meet(tile, ar, send, recv, n, me, device):
        ar[me] = tile
        copies = [remote(ar.at[me], ar.at[me], send.at[o], recv.at[o], device(o)) for o in range(1, n)]
        for copy in copies:
            copy.start()
        return copies

    def add_up(copies, ar, n):
        for copy in copies:
            copy.wait()
        total = ar[0]
        for i in range(1, n):
            total += ar[i]
        return total

    copies = meet(tile, ar1, a1s, a1r, n1, mine1, peer1)
    for s in range(2):
        cols = slice(s * half_c, (s + 1) * half_c)
        usend[:, cols], ussend[:, cols] = code(upd[s])

    def send_u(i, _):
        uscale_copy(i).start()
        u_copy(i).start()
        return 0

    lax.fori_loop(1, NZ, send_u, 0)
    for put in puts[:2]:
        put.start()
    tile = add_up(copies, ar1, n1)
    copies = meet(tile, ar3, a3s, a3r, ny, y, lambda o: {"dp": dp, "tensor": lax.rem(y + o, ny)})
    tile = add_up(copies, ar3, ny)
    copies = meet(tile, ar2, a2s, a2r, NZ, z, zpeer)
    tile = add_up(copies, ar2, NZ)
    norms = jnp.sqrt(jnp.sum(tile, axis=1, keepdims=True))
    ratio = norms[2:4] / (norms[0:2] + 1e-06)
    ratio_ref[...] = jnp.broadcast_to(ratio, ratio_ref.shape)
    move = [jnp.broadcast_to(0.05 * ratio[s:s + 1], (1, half_c)) for s in range(2)]
    for s in range(2):
        new = w_ref[:, s, :] - move[s] * upd[s]
        nw_ref[:, s, :] = new
        ag[dp, :, s * half_c:(s + 1) * half_c] = new.astype(jnp.bfloat16)

    def held(i, p):
        return at(lax.rem(x - p + NX, NX), lax.rem(z - near_shift(i) + NZ, NZ), c)

    def gx_copy(i, p):
        block = held(i, 0)
        return remote(ag.at[block], ag.at[block], gxs.at[i, p], gxr.at[i, p], xpeer(p))

    def gc_copy(i, p):
        block = held(i, p)
        return remote(ag.at[block], ag.at[block], gcs.at[i, p], gcr.at[i, p], partner)

    def send_x(i, _):
        @pl.when(i > 0)
        def _():
            w_copy(i).wait_recv()
            uscale_copy(i).wait_recv()
            u_copy(i).wait_recv()
            block = held(i, 0)
            for s in range(2):
                cols = slice(s * half_c, (s + 1) * half_c)
                new = wz[i, :, s, :] - move[s] * decode(uz[i, :, cols], uzs[i, :, cols])
                ag[block, :, cols] = new.astype(jnp.bfloat16)

        for p in (1, 3, 2) if NX == 4 else range(1, NX):
            gx_copy(i, p).start()
        gc_copy(i, 0).start()
        return 0

    lax.fori_loop(0, NZ, send_x, 0)
    for put in puts[2:4]:
        put.start()
    acc[...] = jnp.zeros_like(acc)

    def gather(i, _):
        @pl.when(i < NZ)
        def _():
            for p in range(1, NX):
                gx_copy(i, p).wait_recv()
                gc_copy(i, p).start()

        @pl.when(i >= LAG_CORE)
        def _():
            j = i - LAG_CORE
            for p in range(NX):
                gc_copy(j, p).wait_recv()
            zz = lax.rem(z - near_shift(j) + NZ, NZ)
            cols = [pl.ds(pl.multiple_of((bx * NZ + zz) * wide, wide), wide) for bx in range(NX)]
            left = jnp.concatenate([act[:, at_] for at_ in cols], axis=1)
            right = jnp.concatenate([ag[at(bx, zz, cc)] for bx in range(NX) for cc in range(NC)], axis=0)
            acc[...] += jnp.dot(left, right, preferred_element_type=f32)

        return 0

    lax.fori_loop(0, NZ + LAG_CORE, gather, 0)
    kv_ref[:, 0, :] = acc[:, :half_c].astype(jnp.bfloat16)
    kv_ref[:, 1, :] = acc[:, half_c:].astype(jnp.bfloat16)

    puts[4].start()

    def drain(k, _):
        core_copy(k).wait_send()
        for o in range(1, NX):
            xscale_copy(k, o).wait_send()
            x_copy(k, o).wait_send()
            gx_copy(k, o).wait_send()
        for p in range(NX):
            gc_copy(k, p).wait_send()

        @pl.when(k < NZ - 1)
        def _():
            z_copy(k).wait_send()
            zscale_copy(k).wait_send()

        @pl.when(k > 0)
        def _():
            w_copy(k).wait_send()
            u_copy(k).wait_send()
            uscale_copy(k).wait_send()

        return 0

    lax.fori_loop(0, NZ, drain, 0)
    for put in puts:
        put.wait()


def local(ny, activations, grad_out, weights, first_moment, second_moment, step):
    tokens, d = activations.shape
    half_c = grad_out.shape[2]
    cols = 2 * half_c
    rows = d // (NX * NZ * NC)
    f32, bf16 = jnp.float32, jnp.bfloat16
    vmem, dma = pltpu.VMEM, pltpu.SemaphoreType.DMA
    any_, in_vmem = pl.BlockSpec(memory_space=pl.ANY), pl.BlockSpec(memory_space=pltpu.VMEM)
    state = jax.ShapeDtypeStruct((rows, 2, half_c), f32)
    nw, nm, nv, ratio, kv = pl.pallas_call(
        functools.partial(fresh, ny, rows),
        name="lamb_kv",
        out_shape=(state, state, state, jax.ShapeDtypeStruct((2, half_c), f32),
                   jax.ShapeDtypeStruct((tokens, 2, half_c), bf16)),
        in_specs=[pl.BlockSpec(memory_space=pltpu.SMEM)] + [any_] * 5,
        out_specs=(any_,) * 5,
        scratch_shapes=[
            vmem((rows, 2, half_c), f32),
            vmem((rows, 2, half_c), f32),
            vmem((rows, 2, half_c), f32),
            vmem((2, half_c), f32),
            vmem((tokens, 2, half_c), bf16),
            vmem((tokens, d), bf16),
            vmem((tokens, 2, half_c), bf16),
            vmem((rows, 2, half_c), f32),
            vmem((rows, 2, half_c), f32),
            vmem((rows, 2, half_c), f32),
            vmem((tokens, cols), bf16),
            vmem((NZ, NX, NC * rows, cols), f32),
            vmem((NZ, NX, rows, cols), f32),
            vmem((NZ, NX - 1, rows, cols), jnp.int16),
            vmem((NZ, NX - 1, rows, cols), jnp.int16),
            vmem((NZ, NX - 1, 1, cols), f32),
            vmem((NZ, NX - 1, 1, cols), f32),
            vmem((NZ, rows, cols), jnp.int16),
            vmem((NZ, rows, cols), jnp.int16),
            vmem((NZ, 1, cols), f32),
            vmem((NZ, 1, cols), f32),
            vmem((rows, cols), f32),
            vmem((2, rows, half_c), f32),
            vmem((NZ, rows, 2, half_c), f32),
            vmem((rows, cols), jnp.int16),
            vmem((1, cols), f32),
            vmem((NZ, rows, cols), jnp.int16),
            vmem((NZ, 1, cols), f32),
            vmem((NX * NC, 8, half_c), f32),
            vmem((NZ, 8, half_c), f32),
            vmem((ny, 8, half_c), f32),
            vmem((NX * NZ * NC, rows, cols), bf16),
            vmem((tokens, cols), f32),
            dma((NZ, NX)), dma((4,)), dma((5,)), dma((NZ,)), dma((NZ,)),
            dma((NZ, NX - 1)), dma((NZ, NX - 1)), dma((NZ, NX - 1)), dma((NZ, NX - 1)),
            dma((NZ,)), dma((NZ,)), dma((NZ,)), dma((NZ,)),
            dma((NX * NC,)), dma((NX * NC,)), dma((NZ,)), dma((NZ,)), dma((ny,)), dma((ny,)),
            dma((NZ,)), dma((NZ,)), dma((NZ,)), dma((NZ,)), dma((NZ,)), dma((NZ,)),
            dma((NZ, NX)), dma((NZ, NX)), dma((NZ, NX)), dma((NZ, NX)),
        ],
        compiler_params=pltpu.CompilerParams(collective_id=0, has_side_effects=True, vmem_limit_bytes=56 * 2**20),
    )(step, activations, grad_out, weights, first_moment, second_moment)
    shapes = (state, state, state, jax.ShapeDtypeStruct((tokens, 2, half_c), bf16))
    nw, nm, nv, kv, ratio = pl.pallas_call(
        hand_over,
        name="hand_over",
        out_shape=shapes + (jax.ShapeDtypeStruct((2,), f32),),
        in_specs=[any_] * 4 + [any_],
        out_specs=(any_,) * 4 + (in_vmem,),
        scratch_shapes=[vmem(a.shape, a.dtype) for a in shapes] + [vmem((2, half_c), f32), dma((5,)), dma((4,))],
        compiler_params=pltpu.CompilerParams(vmem_limit_bytes=56 * 2**20),
    )(nw, nm, nv, kv, ratio)
    return nw, nm, nv, ratio, kv


def hand_over(nw, nm, nv, kv, ratio, nw_out, nm_out, nv_out, kv_out, ratio_out, b0, b1, b2, b3, tile, into, out):
    given, bufs, outs = (kv, nw, nm, nv), (b3, b0, b1, b2), (kv_out, nw_out, nm_out, nv_out)
    ins = [pltpu.make_async_copy(g, b, into.at[i]) for i, (g, b) in enumerate(zip(given, bufs))]
    last = pltpu.make_async_copy(ratio, tile, into.at[4])
    for copy in ins:
        copy.start()
    last.start()
    puts = [pltpu.make_async_copy(b, o, out.at[i]) for i, (b, o) in enumerate(zip(bufs, outs))]
    for copy, put in zip(ins, puts):
        copy.wait()
        put.start()
    last.wait()
    ratio_out[...] = jnp.max(tile[...], axis=1)
    for put in puts:
        put.wait()


def solution(mesh):
    in_specs = (
        P("dp", None),
        P("dp", None, "tensor"),
        P("dp", None, "tensor"),
        P("dp", None, "tensor"),
        P("dp", None, "tensor"),
        P(),
    )
    out_specs = (
        P("dp", None, "tensor"),
        P("dp", None, "tensor"),
        P("dp", None, "tensor"),
        P(),
        P("dp", None, "tensor"),
    )
    return jax.shard_map(functools.partial(local, mesh.shape["tensor"]), mesh=mesh, in_specs=in_specs,
                         out_specs=out_specs, check_vma=False)
```

```python
import functools
import math

import jax
import jax.numpy as jnp
from jax import lax
from jax.experimental import pallas as pl
from jax.experimental.pallas import tpu as pltpu
from jax.sharding import PartitionSpec as P

NX, NZ, NC = 4, 8, 2
MESH = pl.DeviceIdType.MESH
TOP = 32767.0
MEET, LAG = 0, 3
LAG_CORE = 2
LAG_X = 3


def code(value):
    top = jnp.max(jnp.abs(value), axis=0, keepdims=True)
    return jnp.round(value * (TOP / jnp.maximum(top, 1e-30))).astype(jnp.int32).astype(jnp.int16), top


def decode(short, top):
    return short.astype(jnp.int32).astype(jnp.float32) * (top * (1.0 / TOP))


def chunk_shift(k):
    half = NZ // 2
    return lax.select(lax.rem(k, 2) == 1, half - (k + 1) // 2, half + k // 2)


def near_shift(i):
    return lax.select(lax.rem(i, 2) == 1, (i + 1) // 2, lax.rem(NZ - i // 2, NZ))


def fresh(ny, rows, step_ref, act_hbm, gout_hbm, w_hbm, m_hbm, v_hbm,
          nw_out, nm_out, nv_out, ratio_out, kv_out,
          nw_ref, nm_ref, nv_ref, ratio_ref, kv_ref,
          act, gout, w_ref, m_ref, v_ref, g2, mm, crecv, fsend, frecv, fssend, fsrecv, xsend, xrecv, xssend, xsrecv, zsend, zrecv, zssend, zsrecv, own,
          upd, wz, usend, ussend, uz, uzs, ar1, ar2, ar3, ag, acc,
          act_sem, in_sem, out_sem, cs, cr, fs, fr, fss, fsr, xs, xr, xss, xsr, zs, zr, zss, zsr, a1s, a1r, a2s, a2r, a3s, a3r,
          ws, wr, us, ur, uss, usr, gxs, gxr, gfs, gfr, gcs, gcr):
    dp, y = lax.axis_index("dp"), lax.axis_index("tensor")
    c = lax.rem(dp, NC)
    z = lax.rem(dp // NC, NZ)
    x = dp // (NC * NZ)
    wide, part_rows = NC * rows, rows // 2
    f32 = jnp.float32

    def at(xx, zz, cc):
        return (xx * NZ + zz) * NC + cc

    def dev(index):
        return {"dp": index, "tensor": y}

    def remote(src, dst, send, recv, device):
        return pltpu.make_async_remote_copy(src_ref=src, dst_ref=dst, send_sem=send, recv_sem=recv,
                                            device_id=device, device_id_type=MESH)

    partner = dev(at(x, z, 1 - c))

    def xpeer(o):
        return dev(at(lax.rem(x + o, NX), z, c))

    def zpeer(o):
        return dev(at(x, lax.rem(z + o, NZ), c))

    load_g = pltpu.make_async_copy(gout_hbm, gout, in_sem.at[0])
    load_w = pltpu.make_async_copy(w_hbm, w_ref, in_sem.at[1])
    load_m = pltpu.make_async_copy(m_hbm, m_ref, in_sem.at[2])
    load_v = pltpu.make_async_copy(v_hbm, v_ref, in_sem.at[3])

    def strip(bx, k):
        zz = lax.rem(z + chunk_shift(k), NZ)
        return pl.ds(pl.multiple_of((bx * NZ + zz) * wide, wide), wide)

    def load_act(bx, k):
        return pltpu.make_async_copy(act_hbm.at[:, strip(bx, k)], act.at[:, strip(bx, k)], act_sem.at[k, bx])

    load_g.start()

    def start_loads(k, _):
        for bx in range(NX):
            load_act(bx, k).start()
        return 0

    lax.fori_loop(0, NZ, start_loads, 0)
    load_w.start()
    load_m.start()
    load_v.start()
    barrier = pltpu.get_barrier_semaphore()

    def greet(device):
        pl.semaphore_signal(barrier, inc=1, device_id=device, device_id_type=MESH)

    mine1 = x * NC + c
    n1 = NX * NC

    def peer1(o):
        other = lax.rem(mine1 + o, n1)
        return dev(at(other // NC, z, lax.rem(other, NC)))

    for o in range(1, n1):
        greet(peer1(o))
    for o in range(1, NZ):
        greet(zpeer(o))
    for o in range(1, ny):
        greet({"dp": dp, "tensor": lax.rem(y + o, ny)})
    greeted = n1 - 1 + NZ - 1 + ny - 1

    load_g.wait()
    half_c = g2.shape[1] // 2
    g2[:, :half_c] = gout[:, 0, :]
    g2[:, half_c:] = gout[:, 1, :]

    own_rows = pl.ds(pl.multiple_of(c * rows, rows), rows)
    other_rows = pl.ds(pl.multiple_of((1 - c) * rows, rows), rows)

    def core_copy(k):
        return remote(mm.at[k, :, other_rows, :], crecv.at[k], cs.at[k], cr.at[k], partner)

    beside = (1, NX - 1)

    def far_copies(k, way):
        to = xpeer(beside[way])
        return (remote(fssend.at[k], fsrecv.at[k, way], fss.at[k, way], fsr.at[k, way], to),
                remote(fsend.at[k, way], frecv.at[k, way], fs.at[k, way], fr.at[k, way], to))

    def near_copies(k, way):
        to = xpeer(beside[way])
        return (remote(xssend.at[k, way], xsrecv.at[k, way], xss.at[k, way], xsr.at[k, way], to),
                remote(xsend.at[k, way], xrecv.at[k, way], xs.at[k, way], xr.at[k, way], to))

    def start(copies):
        for copy in copies:
            copy.start()

    def arrive(copies):
        for copy in copies:
            copy.wait_recv()

    def left(copies):
        for copy in copies:
            copy.wait_send()

    def z_copy(k):
        return remote(zsend.at[k], zrecv.at[k], zs.at[k], zr.at[k], zpeer(chunk_shift(k)))

    def zscale_copy(k):
        return remote(zssend.at[k], zsrecv.at[k], zss.at[k], zsr.at[k], zpeer(chunk_shift(k)))

    def w_copy(i):
        return remote(w_ref if i < 3 else wz.at[i - 2], wz.at[i], ws.at[i], wr.at[i], zpeer(1 if i % 2 else NZ - 1))

    def pass_w(turn):
        for i in (2 * turn + 1, 2 * turn + 2):
            if i + 2 < NZ:
                w_copy(i).wait_recv()
                w_copy(i + 2).start()

    def u_copy(i):
        return remote(usend, uz.at[i], us.at[i], ur.at[i], zpeer(near_shift(i)))

    def uscale_copy(i):
        return remote(ussend, uzs.at[i], uss.at[i], usr.at[i], zpeer(near_shift(i)))

    def grads(k, _):
        @pl.when(k < NZ)
        def _():
            for bx in range(NX):
                load_act(bx, k).wait()
            strips = jnp.concatenate([act[:, strip(bx, k)] for bx in range(NX)], axis=1)
            part = lax.dot_general(strips, g2[...], (((0,), (0,)), ((), ())), preferred_element_type=f32)
            for bx in range(NX):
                mm[k, bx] = part[bx * wide:(bx + 1) * wide]

            @pl.when(k == MEET)
            def _():
                pl.semaphore_wait(barrier, greeted)
                for j in range(MEET):
                    core_copy(j).start()

            @pl.when(k >= MEET)
            def _():
                core_copy(k).start()

            @pl.when(k == MEET)
            def _():
                load_w.wait()
                for i in range(1, min(3, NZ)):
                    w_copy(i).start()

        @pl.when(k >= LAG)
        def _():
            j = k - LAG
            core_copy(j).wait_recv()
            bx = lax.rem(x + NX // 2, NX)
            short, fssend[j] = code(mm[j, bx, own_rows, :] + crecv[j, bx])
            for way in range(2):
                fsend[j, way] = short[way * part_rows:(way + 1) * part_rows]
                start(far_copies(j, way))

        return 0

    lax.fori_loop(0, NZ + LAG, grads, 0)

    def along_x(i, _):
        @pl.when(i < NZ)
        def _():
            for way in range(2):
                bx = lax.rem(x + beside[way], NX)
                value = mm[i, bx, own_rows, :] + crecv[i, bx]
                arrive(far_copies(i, way))
                more = decode(frecv[i, way], fsrecv[i, way])
                low, high = value[:part_rows], value[part_rows:]
                value = jnp.concatenate([low, high + more] if way else [low + more, high], axis=0)
                xsend[i, way], xssend[i, way] = code(value)
                start(near_copies(i, way))

        @pl.when(i >= LAG_X)
        def _():
            k = i - LAG_X
            total = mm[k, x, own_rows, :] + crecv[k, x]
            for way in range(2):
                arrive(near_copies(k, way))
                total += decode(xrecv[k, way], xsrecv[k, way])

            @pl.when(k < NZ - 1)
            def _():
                zsend[k], zssend[k] = code(total)
                zscale_copy(k).start()
                z_copy(k).start()

            @pl.when(k == NZ - 1)
            def _():
                own[...] = total

        return 0

    lax.fori_loop(0, NZ + LAG_X, along_x, 0)
    pass_w(0)

    load_m.wait()
    load_v.wait()
    count = jnp.full((1, half_c), step_ref[0].astype(f32), f32)
    bias_one = 1.0 - jnp.exp(count * math.log(0.9))
    bias_two = 1.0 - jnp.exp(count * math.log(0.95))

    def along_z(k, total):
        zscale_copy(k).wait_recv()
        z_copy(k).wait_recv()
        return total + decode(zrecv[k], zsrecv[k])

    grad = lax.fori_loop(0, NZ - 1, along_z, own[...])

    sums_u, sums_w = [], []
    for s in range(2):
        g = grad[:, s * half_c:(s + 1) * half_c]
        weight = w_ref[:, s, :]
        first = 0.9 * m_ref[:, s, :] + 0.1 * g
        second = 0.95 * v_ref[:, s, :] + 0.05 * g * g
        update = first / bias_one / (jnp.sqrt(second / bias_two) + 1e-06) + 0.1 * weight
        nm_ref[:, s, :] = first
        nv_ref[:, s, :] = second
        upd[s] = update
        sums_u.append(jnp.sum(update * update, axis=0, keepdims=True))
        sums_w.append(jnp.sum(weight * weight, axis=0, keepdims=True))
    puts = [pltpu.make_async_copy(a, b, out_sem.at[i]) for i, (a, b) in enumerate(
        ((nm_ref, nm_out), (nv_ref, nv_out), (nw_ref, nw_out), (ratio_ref, ratio_out), (kv_ref, kv_out)))]
    tile = jnp.concatenate(sums_u + sums_w + [jnp.zeros((4, half_c), f32)], axis=0)

    def meet(tile, ar, send, recv, n, me, device):
        ar[me] = tile
        copies = [remote(ar.at[me], ar.at[me], send.at[o], recv.at[o], device(o)) for o in range(1, n)]
        for copy in copies:
            copy.start()
        return copies

    def add_up(copies, ar, n):
        for copy in copies:
            copy.wait()
        total = ar[0]
        for i in range(1, n):
            total += ar[i]
        return total

    copies = meet(tile, ar1, a1s, a1r, n1, mine1, peer1)
    for s in range(2):
        cols = slice(s * half_c, (s + 1) * half_c)
        usend[:, cols], ussend[:, cols] = code(upd[s])

    def send_u(i, _):
        uscale_copy(i).start()
        u_copy(i).start()
        return 0

    lax.fori_loop(1, NZ, send_u, 0)
    for put in puts[:2]:
        put.start()
    pass_w(1)
    tile = add_up(copies, ar1, n1)
    copies = meet(tile, ar3, a3s, a3r, ny, y, lambda o: {"dp": dp, "tensor": lax.rem(y + o, ny)})
    tile = add_up(copies, ar3, ny)
    pass_w(2)
    copies = meet(tile, ar2, a2s, a2r, NZ, z, zpeer)
    tile = add_up(copies, ar2, NZ)
    norms = jnp.sqrt(jnp.sum(tile, axis=1, keepdims=True))
    ratio = norms[2:4] / (norms[0:2] + 1e-06)
    ratio_ref[...] = jnp.broadcast_to(ratio, ratio_ref.shape)
    move = [jnp.broadcast_to(0.05 * ratio[s:s + 1], (1, half_c)) for s in range(2)]
    for s in range(2):
        new = w_ref[:, s, :] - move[s] * upd[s]
        nw_ref[:, s, :] = new
        ag[dp, :, s * half_c:(s + 1) * half_c] = new.astype(jnp.bfloat16)

    def held(i, p):
        return at(lax.rem(x - p + NX, NX), lax.rem(z - near_shift(i) + NZ, NZ), c)

    def gx_copy(i, p):
        block = held(i, 0)
        return remote(ag.at[block], ag.at[block], gxs.at[i, p], gxr.at[i, p], xpeer(p))

    def gf_copy(i, way):
        ref = ag.at[held(i, beside[way]), pl.ds(way * part_rows, part_rows)]
        return remote(ref, ref, gfs.at[i, way], gfr.at[i, way], xpeer(beside[way]))

    def gc_copy(i, p):
        block = held(i, p)
        return remote(ag.at[block], ag.at[block], gcs.at[i, p], gcr.at[i, p], partner)

    def send_x(i, _):
        @pl.when(i > 0)
        def _():
            for last in range(max(1, NZ - 2), NZ):
                @pl.when(i == last)
                def _(last=last):
                    w_copy(last).wait_recv()

            uscale_copy(i).wait_recv()
            u_copy(i).wait_recv()
            block = held(i, 0)
            for s in range(2):
                cols = slice(s * half_c, (s + 1) * half_c)
                new = wz[i, :, s, :] - move[s] * decode(uz[i, :, cols], uzs[i, :, cols])
                ag[block, :, cols] = new.astype(jnp.bfloat16)

        for p in beside:
            gx_copy(i, p).start()
        gc_copy(i, 0).start()
        return 0

    lax.fori_loop(0, NZ, send_x, 0)
    for put in puts[2:4]:
        put.start()
    acc[...] = jnp.zeros_like(acc)

    def product(j, shifts):
        zz = lax.rem(z - near_shift(j) + NZ, NZ)
        places = [lax.rem(x - p + NX, NX) for p in shifts]
        cols = [pl.ds(pl.multiple_of((bx * NZ + zz) * wide, wide), wide) for bx in places]
        rows_in = jnp.concatenate([act[:, at_] for at_ in cols], axis=1)
        right = jnp.concatenate([ag[at(bx, zz, cc)] for bx in places for cc in range(NC)], axis=0)
        acc[...] += jnp.dot(rows_in, right, preferred_element_type=f32)

    half_way = NX // 2

    def gather(i, _):
        @pl.when(i < NZ)
        def _():
            for way in range(2):
                gx_copy(i, beside[way]).wait_recv()
                gf_copy(i, way).start()
                gc_copy(i, beside[way]).start()

        @pl.when((i >= NZ) & (i < 2 * NZ))
        def _():
            for way in range(2):
                gf_copy(i - NZ, way).wait_recv()
            gc_copy(i - NZ, half_way).start()

        @pl.when((i >= LAG_CORE) & (i < NZ + LAG_CORE))
        def _():
            j = i - LAG_CORE
            for p in (0,) + beside:
                gc_copy(j, p).wait_recv()
            product(j, (0,) + beside)

        @pl.when(i >= NZ + LAG_CORE)
        def _():
            j = i - NZ - LAG_CORE
            gc_copy(j, half_way).wait_recv()
            product(j, (half_way,))

        return 0

    lax.fori_loop(0, 2 * NZ + LAG_CORE, gather, 0)
    kv_ref[...] = acc[...].reshape(kv_ref.shape).astype(jnp.bfloat16)

    puts[4].start()

    def drain(k, _):
        core_copy(k).wait_send()
        for way in range(2):
            left(far_copies(k, way))
            left(near_copies(k, way))
            gx_copy(k, beside[way]).wait_send()
            gf_copy(k, way).wait_send()
        for p in range(NX):
            gc_copy(k, p).wait_send()

        @pl.when(k < NZ - 1)
        def _():
            z_copy(k).wait_send()
            zscale_copy(k).wait_send()

        @pl.when(k > 0)
        def _():
            u_copy(k).wait_send()
            uscale_copy(k).wait_send()

        return 0

    for i in range(1, NZ):
        w_copy(i).wait_send()
    lax.fori_loop(0, NZ, drain, 0)
    for put in puts:
        put.wait()


def local(ny, activations, grad_out, weights, first_moment, second_moment, step):
    tokens, d = activations.shape
    half_c = grad_out.shape[2]
    cols = 2 * half_c
    rows = d // (NX * NZ * NC)
    f32, bf16 = jnp.float32, jnp.bfloat16
    vmem, dma = pltpu.VMEM, pltpu.SemaphoreType.DMA
    any_, in_vmem = pl.BlockSpec(memory_space=pl.ANY), pl.BlockSpec(memory_space=pltpu.VMEM)
    state = jax.ShapeDtypeStruct((rows, 2, half_c), f32)
    nw, nm, nv, ratio, kv = pl.pallas_call(
        functools.partial(fresh, ny, rows),
        name="lamb_kv",
        out_shape=(state, state, state, jax.ShapeDtypeStruct((2, half_c), f32),
                   jax.ShapeDtypeStruct((tokens, 2, half_c), bf16)),
        in_specs=[pl.BlockSpec(memory_space=pltpu.SMEM)] + [any_] * 5,
        out_specs=(any_,) * 5,
        scratch_shapes=[
            vmem((rows, 2, half_c), f32),
            vmem((rows, 2, half_c), f32),
            vmem((rows, 2, half_c), f32),
            vmem((2, half_c), f32),
            vmem((tokens, 2, half_c), bf16),
            vmem((tokens, d), bf16),
            vmem((tokens, 2, half_c), bf16),
            vmem((rows, 2, half_c), f32),
            vmem((rows, 2, half_c), f32),
            vmem((rows, 2, half_c), f32),
            vmem((tokens, cols), bf16),
            vmem((NZ, NX, NC * rows, cols), f32),
            vmem((NZ, NX, rows, cols), f32),
            vmem((NZ, 2, rows // 2, cols), jnp.int16),
            vmem((NZ, 2, rows // 2, cols), jnp.int16),
            vmem((NZ, 1, cols), f32),
            vmem((NZ, 2, 1, cols), f32),
            vmem((NZ, 2, rows, cols), jnp.int16),
            vmem((NZ, 2, rows, cols), jnp.int16),
            vmem((NZ, 2, 1, cols), f32),
            vmem((NZ, 2, 1, cols), f32),
            vmem((NZ, rows, cols), jnp.int16),
            vmem((NZ, rows, cols), jnp.int16),
            vmem((NZ, 1, cols), f32),
            vmem((NZ, 1, cols), f32),
            vmem((rows, cols), f32),
            vmem((2, rows, half_c), f32),
            vmem((NZ, rows, 2, half_c), f32),
            vmem((rows, cols), jnp.int16),
            vmem((1, cols), f32),
            vmem((NZ, rows, cols), jnp.int16),
            vmem((NZ, 1, cols), f32),
            vmem((NX * NC, 8, half_c), f32),
            vmem((NZ, 8, half_c), f32),
            vmem((ny, 8, half_c), f32),
            vmem((NX * NZ * NC, rows, cols), bf16),
            vmem((tokens, cols), f32),
            dma((NZ, NX)), dma((4,)), dma((5,)), dma((NZ,)), dma((NZ,)),
            dma((NZ, 2)), dma((NZ, 2)), dma((NZ, 2)), dma((NZ, 2)), dma((NZ, 2)), dma((NZ, 2)), dma((NZ, 2)), dma((NZ, 2)),
            dma((NZ,)), dma((NZ,)), dma((NZ,)), dma((NZ,)),
            dma((NX * NC,)), dma((NX * NC,)), dma((NZ,)), dma((NZ,)), dma((ny,)), dma((ny,)),
            dma((NZ,)), dma((NZ,)), dma((NZ,)), dma((NZ,)), dma((NZ,)), dma((NZ,)),
            dma((NZ, NX)), dma((NZ, NX)), dma((NZ, 2)), dma((NZ, 2)), dma((NZ, NX)), dma((NZ, NX)),
        ],
        compiler_params=pltpu.CompilerParams(collective_id=0, has_side_effects=True, vmem_limit_bytes=56 * 2**20),
    )(step, activations, grad_out, weights, first_moment, second_moment)
    shapes = (state, state, state, jax.ShapeDtypeStruct((tokens, 2, half_c), bf16))
    nw, nm, nv, kv, ratio = pl.pallas_call(
        hand_over,
        name="hand_over",
        out_shape=shapes + (jax.ShapeDtypeStruct((2,), f32),),
        in_specs=[any_] * 4 + [any_],
        out_specs=(any_,) * 4 + (in_vmem,),
        scratch_shapes=[vmem(a.shape, a.dtype) for a in shapes] + [vmem((2, half_c), f32), dma((5,)), dma((4,))],
        compiler_params=pltpu.CompilerParams(vmem_limit_bytes=56 * 2**20),
    )(nw, nm, nv, kv, ratio)
    return nw, nm, nv, ratio, kv


def hand_over(nw, nm, nv, kv, ratio, nw_out, nm_out, nv_out, kv_out, ratio_out, b0, b1, b2, b3, tile, into, out):
    given, bufs, outs = (kv, nw, nm, nv), (b3, b0, b1, b2), (kv_out, nw_out, nm_out, nv_out)
    ins = [pltpu.make_async_copy(g, b, into.at[i]) for i, (g, b) in enumerate(zip(given, bufs))]
    last = pltpu.make_async_copy(ratio, tile, into.at[4])
    for copy in ins:
        copy.start()
    last.start()
    puts = [pltpu.make_async_copy(b, o, out.at[i]) for i, (b, o) in enumerate(zip(bufs, outs))]
    for copy, put in zip(ins, puts):
        copy.wait()
        put.start()
    last.wait()
    ratio_out[...] = jnp.max(tile[...], axis=1)
    for put in puts:
        put.wait()


def solution(mesh):
    in_specs = (
        P("dp", None),
        P("dp", None, "tensor"),
        P("dp", None, "tensor"),
        P("dp", None, "tensor"),
        P("dp", None, "tensor"),
        P(),
    )
    out_specs = (
        P("dp", None, "tensor"),
        P("dp", None, "tensor"),
        P("dp", None, "tensor"),
        P(),
        P("dp", None, "tensor"),
    )
    return jax.shard_map(functools.partial(local, mesh.shape["tensor"]), mesh=mesh, in_specs=in_specs,
                         out_specs=out_specs, check_vma=False)
```
